128 devices in a mesh: dp: 16 (over y, z), mp: 8 (over x, core).
Axes of the slice: x: 4, y: 4, z: 4, core: 2. Of those that a mesh axis runs over, the one named last changes fastest.
Arguments:
- activations: bfloat16 [4, 8192, 5120], P(None, 'dp'), may hold values from -60 to 60
- task_weights: bfloat16 [4, 5120, 1024], P(None, 'dp', 'mp'), may hold values from -6 to 6
Outputs:
- merged: float32 [5120, 1024], P('dp', 'mp')
The draws below stay inside these ranges and needn't reach their ends.
All inputs are finite; a program needn't handle non-finite values.
Results may differ from the reference program's by a relative error of at most 0.0015.
Values may be sent and summed in bfloat16 or wider, within the bound.
No kernel may reach another device: no remote copies, remote signals or barrier semaphores. Data moves between devices by JAX's collectives and lax.ppermute only.
A program may use at most 128 MiB of HBM per device.

```python
import math
import jax
import jax.numpy as jnp
from jax import lax

D = 5120
TASKS = 4
ITERS = 2
TOK_TASK = 8192
SLAB = 1024


def draw_activations(key, part):
    key_feat = jax.random.fold_in(key, 11)
    key_tok = jax.random.fold_in(key, 12)
    key_base = jax.random.fold_in(key, 13)
    feature_scale = jnp.exp(jax.random.uniform(key_feat, (TASKS, 1, D), jnp.float32, 0.0, math.log(10.0)))
    token_scale = jnp.exp(jax.random.uniform(key_tok, (TASKS, TOK_TASK, 1), jnp.float32, 0.0, math.log(3.0)))
    base = jnp.clip(jax.random.normal(key_base, (TASKS, TOK_TASK, D), jnp.float32), -6.0, 6.0)
    return (base * feature_scale * token_scale / 3.0).astype(jnp.bfloat16)


def level_of(key, extent, cuts, least, top_value):
    factor_of = 1.0
    for axis_at, blocks in cuts:
        steps = jax.random.uniform(jax.random.fold_in(jax.random.fold_in(key, 6), axis_at), (blocks,), jnp.float32, least / len(cuts), top_value / len(cuts))
        factor_of = factor_of * jnp.repeat(jnp.exp(steps), extent[axis_at] // blocks).reshape((-1,) + (1,) * (len(extent) - 1 - axis_at))
    return factor_of


def gaussian(own_key, shape, deviation, reach, split=(), dtype=jnp.bfloat16):
    array = deviation * jax.random.normal(own_key, shape, jnp.float32)
    if split:
        array = array * level_of(own_key, shape, split, -0.22, 0.18)
    return jnp.clip(array, -reach, reach).astype(dtype)


def setup_inputs(seed: int = 0) -> dict:
    key_of = jax.random.split(jax.random.key(seed), 3)
    activations = draw_activations(jax.random.fold_in(key_of[2], 71), 0)
    task_weights = gaussian(key_of[1], (TASKS, D, SLAB), 1.0, 6.0, ((1, 16), (2, 8)))
    return dict(activations=activations, task_weights=task_weights)


ALPHA = 0.9


def reference(activations, task_weights):
    total = TASKS * TOK_TASK
    flat = activations.reshape(-1, D)
    gram = jnp.dot(flat.T, flat, preferred_element_type=jnp.float32) / total
    row_ids = lax.broadcasted_iota(jnp.int32, (D, D), 0)
    col_ids = lax.broadcasted_iota(jnp.int32, (D, D), 1)
    operator = jnp.where(row_ids == col_ids, gram, ALPHA * gram)
    cross = jnp.zeros((D, SLAB), jnp.float32)
    diag_part = jnp.zeros((D, SLAB), jnp.float32)
    for task in range(TASKS):
        outputs = jnp.dot(activations[task], task_weights[task], preferred_element_type=jnp.float32).astype(jnp.bfloat16)
        cross = cross + jnp.dot(activations[task].T, outputs, preferred_element_type=jnp.float32)
        squares = jnp.sum(activations[task].astype(jnp.float32) ** 2, axis=0)
        diag_part = diag_part + squares[:, None] * task_weights[task].astype(jnp.float32)
    target = (ALPHA * cross + (1.0 - ALPHA) * diag_part) / total

    def apply(vector):
        return jnp.dot(operator, vector, precision=lax.Precision.HIGHEST)

    merged = jnp.mean(task_weights.astype(jnp.float32), axis=0)
    residual = target - apply(merged)
    direction = residual
    norm_now = jnp.sum(residual * residual, axis=0)
    for step in range(ITERS):
        image = apply(direction)
        alpha = norm_now / jnp.sum(direction * image, axis=0)
        merged = merged + alpha * direction
        if step + 1 < ITERS:
            residual = residual - alpha * image
            norm_next = jnp.sum(residual * residual, axis=0)
            direction = residual + (norm_next / norm_now) * direction
            norm_now = norm_next
    return merged
```

```python
import functools

import jax
import jax.numpy as jnp
from jax import lax
from jax.experimental import pallas as pl
from jax.experimental.pallas import tpu as pltpu
from jax.sharding import PartitionSpec as P

ALPHA = 0.9
SIDE = 4
CHUNK = 512
F32 = jnp.float32
BF16 = jnp.bfloat16
ALL = ("dp", "mp")


def mat(left, right):
    return lax.dot_general(left, right, (((1,), (0,)), ((), ())), preferred_element_type=F32)


def mat_t(left, right):
    return lax.dot_general(left, right, (((0,), (0,)), ((), ())), preferred_element_type=F32)


def split(value):
    high = value.astype(BF16)
    return high, (value - high.astype(F32)).astype(BF16)


def block(i, size):
    return pl.ds(pl.multiple_of(i * size, size), size)


def load_kernel(x_hbm, x_ref, squares_ref, flat, sem):
    tasks, width = flat.shape
    owners = squares_ref.shape[0]
    local, rows_own = x_ref.shape[0] // tasks, width // owners
    copies = []
    for t in range(tasks):
        copies.append(
            pltpu.make_async_copy(x_hbm.at[t], x_ref.at[pl.ds(t * local, local)], sem.at[t])
        )
        copies[-1].start()
    for t, copy in enumerate(copies):
        copy.wait()

        def body(j, carry, t=t):
            cols = block(j, CHUNK)
            part = x_ref[t * local : (t + 1) * local, cols].astype(F32)
            flat[t : t + 1, cols] = jnp.sum(part * part, axis=0, keepdims=True)
            return carry

        lax.fori_loop(0, width // CHUNK, body, 0)
    squares_ref[...] = jnp.zeros_like(squares_ref)
    lanes = squares_ref.shape[2]
    for j in range(owners):
        for k, at in enumerate(range(0, rows_own, lanes)):
            size = min(lanes, rows_own - at)
            squares_ref[j, k * tasks : (k + 1) * tasks, :size] = flat[
                :, j * rows_own + at : j * rows_own + at + size
            ]


def token_sums(scale, x_ref, z, out_ref):
    owners, _, lanes = out_ref.shape
    rows_own = x_ref.shape[1] // owners
    for j in range(0, owners, 2):
        both = mat_t(x_ref[:, j * rows_own : (j + 2) * rows_own], z[...])
        both = ((both[:, :lanes] + both[:, lanes:]) * scale).astype(BF16)
        out_ref[j, :rows_own] = both[:rows_own]
        out_ref[j + 1, :rows_own] = both[rows_own:]


def fill(w_ref, blocks, sem):
    copies = []
    for i, (piece, across, along) in enumerate(blocks):
        rows_own = piece.shape[1]
        copies.append(
            pltpu.make_async_copy(
                piece, w_ref.at[:, block(owner(across, along), rows_own)], sem.at[i]
            )
        )
        copies[-1].start()
    for copy in copies:
        copy.wait()


def mean_of(tasks, w_ref, rows):
    total = w_ref[0, rows, :].astype(F32)
    for t in range(1, tasks):
        total = total + w_ref[t, rows, :].astype(F32)
    return total / tasks


def products(tasks, x_ref, w_ref, mean, units):
    lanes = w_ref.shape[2]
    size = mean.shape[0] // len(units)
    for i, unit in enumerate(units):
        high, low = split(mean_of(tasks, w_ref, block(unit, size)))
        mean[i * size : (i + 1) * size, :lanes] = high
        mean[i * size : (i + 1) * size, lanes:] = low
    local = x_ref.shape[0] // tasks
    for t in range(tasks):
        rows = slice(t * local, (t + 1) * local)
        both, rest = 0.0, 0.0
        for i, unit in enumerate(units):
            cols, at = block(unit, size), slice(i * size, (i + 1) * size)
            right = jnp.concatenate([w_ref[t, cols, :], mean[at, :lanes]], axis=1)
            both = both + mat(x_ref[rows, cols], right)
            rest = rest + mat(x_ref[rows, cols], mean[at, lanes:])
        yield rows, both[:, :lanes], both[:, lanes:] + rest


def prepare_kernel(tasks, x_ref, *refs):
    *pieces, part_ref, w_ref, mean, sem = refs
    own, line, pairs = pieces[0], pieces[1:SIDE], pieces[SIDE:]
    blocks = [(own, 0, 0)] + [(piece, 0, k + 1) for k, piece in enumerate(line)]
    for i, pair in enumerate(pairs):
        blocks += [(pair.at[k], (1, 3)[i // 2], i % 2 * 2 + k) for k in range(2)]
    fill(w_ref, blocks, sem)
    lanes = w_ref.shape[2]
    for rows, outputs, shift in products(tasks, x_ref, w_ref, mean, units(False)):
        part_ref[rows, :lanes] = outputs
        part_ref[rows, lanes:] = shift


def first_kernel(
    scale, tasks, x_ref, squares_ref, part_ref, w_in, near_ref, wide_ref, out_ref, w_ref, mean, z, sem
):
    del w_in
    blocks = [(piece.at[k], 2, i * 2 + k) for i, piece in enumerate((near_ref, wide_ref)) for k in range(2)]
    fill(w_ref, blocks, sem)
    lanes = out_ref.shape[2]
    for rows, outputs, shift in products(tasks, x_ref, w_ref, mean, units(True)):
        outputs = outputs + part_ref[rows, :lanes]
        shift = shift + part_ref[rows, lanes:]
        high, low = split(outputs.astype(BF16).astype(F32) - shift)
        z[rows, :lanes] = high
        z[rows, lanes:] = low
    token_sums(scale, x_ref, z, out_ref)
    out_ref[:, x_ref.shape[1] // out_ref.shape[0] :] = squares_ref[...].astype(BF16)


def apply_kernel(scale, x_ref, v_ref, out_ref, u_ref, z):
    for i in range(0, x_ref.shape[0], CHUNK):
        rows = slice(i, i + CHUNK)
        u = mat(x_ref[rows, :], v_ref[...])
        u_ref[rows, :] = u
        z[:, rows] = u.T.astype(BF16)
    rows_own = x_ref.shape[1] // out_ref.shape[0]
    for j in range(0, out_ref.shape[0], 2):
        both = mat(z[...], x_ref[:, j * rows_own : (j + 2) * rows_own])
        both = (both * scale).T.astype(BF16)
        out_ref[j] = both[:rows_own]
        out_ref[j + 1] = both[rows_own:]


def sum_parts(parts_ref):
    total = parts_ref[0].astype(F32)
    for j in range(1, parts_ref.shape[0]):
        total = total + parts_ref[j].astype(F32)
    return total


def residual_kernel(total, parts_ref, w_ref, residual_ref, diag_ref, start_ref, out_ref):
    tasks, rows_own, lanes = w_ref.shape
    summed = sum_parts(parts_ref)
    columns = (summed[rows_own:] / total).T
    mean = w_ref[0].astype(F32)
    for t in range(1, tasks):
        mean = mean + w_ref[t].astype(F32)
    mean = mean / tasks
    for k, at in enumerate(range(0, rows_own, lanes)):
        rows = slice(at, min(at + lanes, rows_own))
        size = rows.stop - rows.start
        diag = jnp.zeros((size, lanes), F32)
        own = jnp.zeros((size, lanes), F32)
        for t in range(tasks):
            column = columns[:size, k * tasks + t : k * tasks + t + 1]
            diag = diag + jnp.broadcast_to(column, diag.shape)
            own = own + column * (w_ref[t, rows].astype(F32) - mean[rows])
        residual = summed[rows] + (1.0 - ALPHA) * own
        residual_ref[rows] = residual
        diag_ref[rows] = diag
        for j in range(out_ref.shape[0]):
            out_ref[j, rows] = residual.astype(BF16)
    start_ref[...] = mean


def image_kernel(parts_ref, residual_ref, diag_ref, image_ref, out_ref):
    residual = residual_ref[...]
    lost = residual - residual.astype(BF16).astype(F32)
    image = sum_parts(parts_ref) + diag_ref[...] * ((1.0 - ALPHA) * residual + ALPHA * lost)
    image_ref[...] = image
    for j in range(out_ref.shape[0]):
        out_ref[j] = image.astype(BF16)


def last_kernel(
    scale, x_ref, u_ref, r_ref, q_ref, residual_ref, image_ref, diag_ref, direction_ref, scal_ref, out_ref, v
):
    for i in range(0, x_ref.shape[0], CHUNK):
        v[i : i + CHUNK, :] = mat(x_ref[i : i + CHUNK, :], q_ref[...])
    r = r_ref[...].astype(F32)
    q = q_ref[...].astype(F32)
    norm = jnp.sum(r * r, axis=0, keepdims=True)
    alpha = norm / jnp.sum(r * q, axis=0, keepdims=True)
    r = r_ref[...].astype(F32) - alpha * q_ref[...].astype(F32)
    norm_next = jnp.sum(r * r, axis=0, keepdims=True)
    beta = norm_next / norm
    residual = residual_ref[...]
    direction = residual - alpha * image_ref[...] + beta * residual
    direction_ref[...] = direction
    scal_ref[...] = jnp.zeros_like(scal_ref)
    scal_ref[0:1, :] = alpha
    scal_ref[1:2, :] = norm_next
    shape = scal_ref.shape
    along = (1.0 + beta) * u_ref[...] - alpha * v[...]
    own = jnp.sum((diag_ref[...] * direction * direction).reshape(-1, *shape), axis=0)
    curve = scale * jnp.sum((along * along).reshape(-1, *shape), axis=0) + (1.0 - ALPHA) * own
    for j in range(out_ref.shape[0]):
        out_ref[j] = curve


def merge_kernel(parts_ref, scal_ref, start_ref, residual_ref, direction_ref, out_ref):
    curve = jnp.sum(sum_parts(parts_ref), axis=0, keepdims=True)
    out_ref[...] = (
        start_ref[...]
        + scal_ref[0:1, :] * residual_ref[...]
        + scal_ref[1:2, :] / curve * direction_ref[...]
    )


def call(kernel, name, scratch, out_shape, *args, place=pltpu.VMEM, n_vmem=1, aliases=None):
    vmem = pl.BlockSpec(memory_space=pltpu.VMEM)
    return pl.pallas_call(
        kernel,
        name=name,
        in_specs=[vmem] * n_vmem + [pl.BlockSpec(memory_space=place)] * (len(args) - n_vmem),
        out_specs=jax.tree.map(lambda _: vmem, out_shape),
        out_shape=out_shape,
        scratch_shapes=scratch,
        input_output_aliases=aliases or {},
        compiler_params=pltpu.CompilerParams(vmem_limit_bytes=10 << 20),
    )(*args)


def place():
    dp, odd = lax.axis_index("dp"), lax.axis_index("mp") % 2
    y, z = dp // SIDE, dp % SIDE
    return odd, jnp.where(odd == 0, y, z), jnp.where(odd == 0, z, y)


def owner(across, along):
    odd, at_across, at_along = place()
    a = (at_across - across + SIDE) % SIDE
    b = (at_along - along + SIDE) % SIDE
    return jnp.where(odd == 0, a * SIDE + b, b * SIDE + a)


def units(late):
    odd, across, _ = place()
    far = (across + 2) % SIDE
    even_units = []
    for base in (across, far) if late else ((across + 1) % SIDE, (across + 3) % SIDE):
        even_units += [2 * base, 2 * base + 1]
    pair = far // 2 if late else 1 - far // 2
    return [jnp.where(odd == 0, even_units[i], 2 * i + pair) for i in range(SIDE)]


def send(value, n_cols, across, along):
    pairs = []
    for dp in range(SIDE * SIDE):
        for mp in range(n_cols):
            step_y, step_z = (across, along) if mp % 2 == 0 else (along, across)
            y, z = (dp // SIDE + step_y) % SIDE, (dp % SIDE + step_z) % SIDE
            pairs.append((dp * n_cols + mp, (y * SIDE + z) * n_cols + mp))
    return lax.ppermute(value, ALL, pairs)


def shards(activations, task_weights):
    tasks, local, width = activations.shape
    lanes = task_weights.shape[2]
    n_rows, n_cols = lax.axis_size("dp"), lax.axis_size("mp")
    rows_own = width // n_rows
    tokens = tasks * local
    total = tokens * n_rows

    def exchange(value):
        return lax.all_to_all(value, "dp", 0, 0, tiled=False)

    scale = ALPHA / total
    unit = pltpu.VMEM((width // 2, 2 * lanes), BF16)
    halves = pltpu.VMEM((tokens, 2 * lanes), BF16)
    rows = jax.ShapeDtypeStruct((rows_own, lanes), F32)
    copies = jax.ShapeDtypeStruct((n_rows, rows_own, lanes), BF16)
    small = jax.ShapeDtypeStruct((8, lanes), F32)
    extra = 2 * 8
    line = [send(task_weights, n_cols, 0, k) for k in range(1, SIDE)]
    vmem = pl.BlockSpec(memory_space=pltpu.VMEM)
    x, squares = pl.pallas_call(
        load_kernel,
        name="load",
        in_specs=[pl.BlockSpec(memory_space=pltpu.HBM)],
        out_specs=(vmem, vmem),
        out_shape=(
            pltpu.VMEM((tokens, width), BF16),
            jax.ShapeDtypeStruct((n_rows, extra, lanes), F32),
        ),
        scratch_shapes=[pltpu.VMEM((tasks, width), F32), pltpu.SemaphoreType.DMA((tasks,))],
        compiler_params=pltpu.CompilerParams(vmem_limit_bytes=4 << 20),
    )(pltpu.with_memory_space_constraint(activations, pltpu.HBM))
    *line, squares = lax.optimization_barrier((*line, squares))
    near, wide = jnp.stack([task_weights, line[0]]), jnp.stack(line[1:])
    left_near = send(near, n_cols, 1, 0)
    right_wide = send(wide, n_cols, 3, 0)
    left_wide = send(wide, n_cols, 1, 0)
    right_near = send(near, n_cols, 3, 0)
    far_near = send(left_near, n_cols, 1, 0)
    far_wide = send(right_wide, n_cols, 3, 0)
    part, w = call(
        functools.partial(prepare_kernel, tasks),
        "prepare",
        [unit, pltpu.SemaphoreType.DMA((n_rows - SIDE,))],
        (
            jax.ShapeDtypeStruct((tokens, 2 * lanes), F32),
            jax.ShapeDtypeStruct((tasks, width, lanes), BF16),
        ),
        x,
        task_weights,
        *line,
        left_near,
        left_wide,
        right_near,
        right_wide,
        place=pl.ANY,
    )
    part, _ = call(
        functools.partial(first_kernel, scale, tasks),
        "first",
        [unit, halves, pltpu.SemaphoreType.DMA((SIDE,))],
        (
            jax.ShapeDtypeStruct((n_rows, rows_own + extra, lanes), BF16),
            jax.ShapeDtypeStruct((tasks, width, lanes), BF16),
        ),
        x,
        squares,
        part,
        w,
        far_near,
        far_wide,
        place=pl.ANY,
        n_vmem=4,
        aliases={3: 1},
    )
    residual, diag, start, sent = call(
        functools.partial(residual_kernel, total),
        "residual",
        [],
        (rows, rows, rows, copies),
        exchange(part),
        task_weights,
    )
    r_full = exchange(sent).reshape(width, lanes)
    part, u = call(
        functools.partial(apply_kernel, scale),
        "apply",
        [pltpu.VMEM((lanes, tokens), BF16)],
        (copies, jax.ShapeDtypeStruct((tokens, lanes), F32)),
        x,
        r_full,
    )
    image, sent = call(image_kernel, "image", [], (rows, copies), exchange(part), residual, diag)
    q_full = exchange(sent).reshape(width, lanes)
    direction, scal, curve = call(
        functools.partial(last_kernel, scale),
        "last",
        [pltpu.VMEM((tokens, lanes), F32)],
        (rows, small, jax.ShapeDtypeStruct((n_rows, 8, lanes), F32)),
        x,
        u,
        r_full,
        q_full,
        residual,
        image,
        diag,
    )
    return call(
        merge_kernel, "merge", [], rows, exchange(curve), scal, start, residual, direction
    )


def solution(mesh):
    return jax.shard_map(
        shards,
        mesh=mesh,
        in_specs=(P(None, "dp", None), P(None, "dp", "mp")),
        out_specs=P("dp", "mp"),
        check_vma=False,
    )
```

```python
import functools

import jax
import jax.numpy as jnp
from jax import lax
from jax.experimental import pallas as pl
from jax.experimental.pallas import tpu as pltpu
from jax.sharding import PartitionSpec as P

ALPHA = 0.9
SIDE = 4
CHUNK = 512
F32 = jnp.float32
BF16 = jnp.bfloat16
ALL = ("dp", "mp")


def mat(left, right):
    return lax.dot_general(left, right, (((1,), (0,)), ((), ())), preferred_element_type=F32)


def mat_t(left, right):
    return lax.dot_general(left, right, (((0,), (0,)), ((), ())), preferred_element_type=F32)


def split(value):
    high = value.astype(BF16)
    return high, (value - high.astype(F32)).astype(BF16)


def block(i, size):
    return pl.ds(pl.multiple_of(i * size, size), size)


def load_kernel(x_hbm, x_ref, squares_ref, flat, sem):
    tasks, width = flat.shape
    owners = squares_ref.shape[0]
    local, rows_own = x_ref.shape[0] // tasks, width // owners
    copies = []
    for t in range(tasks):
        copies.append(
            pltpu.make_async_copy(x_hbm.at[t], x_ref.at[pl.ds(t * local, local)], sem.at[t])
        )
        copies[-1].start()
    for t, copy in enumerate(copies):
        copy.wait()

        def body(j, carry, t=t):
            cols = block(j, CHUNK)
            part = x_ref[t * local : (t + 1) * local, cols].astype(F32)
            flat[t : t + 1, cols] = jnp.sum(part * part, axis=0, keepdims=True)
            return carry

        lax.fori_loop(0, width // CHUNK, body, 0)
    squares_ref[...] = jnp.zeros_like(squares_ref)
    lanes = squares_ref.shape[2]
    for j in range(owners):
        for k, at in enumerate(range(0, rows_own, lanes)):
            size = min(lanes, rows_own - at)
            squares_ref[j, k * tasks : (k + 1) * tasks, :size] = flat[
                :, j * rows_own + at : j * rows_own + at + size
            ]


def token_sums(scale, x_ref, z, out_ref):
    owners, _, lanes = out_ref.shape
    rows_own = x_ref.shape[1] // owners
    for j in range(0, owners, 2):
        both = mat_t(x_ref[:, j * rows_own : (j + 2) * rows_own], z[...])
        both = ((both[:, :lanes] + both[:, lanes:]) * scale).astype(BF16)
        out_ref[j, :rows_own] = both[:rows_own]
        out_ref[j + 1, :rows_own] = both[rows_own:]


def fill(w_ref, blocks, sem):
    copies = []
    for i, (piece, across, along) in enumerate(blocks):
        rows_own = piece.shape[1]
        copies.append(
            pltpu.make_async_copy(
                piece, w_ref.at[:, block(owner(across, along), rows_own)], sem.at[i]
            )
        )
        copies[-1].start()
    for copy in copies:
        copy.wait()


def mean_of(tasks, w_ref, rows):
    total = w_ref[0, rows, :].astype(F32)
    for t in range(1, tasks):
        total = total + w_ref[t, rows, :].astype(F32)
    return total / tasks


def products(tasks, x_ref, w_ref, mean, units):
    lanes = w_ref.shape[2]
    size = mean.shape[0] // len(units)
    for i, unit in enumerate(units):
        high, low = split(mean_of(tasks, w_ref, block(unit, size)))
        mean[i * size : (i + 1) * size, :lanes] = high
        mean[i * size : (i + 1) * size, lanes:] = low
    local = x_ref.shape[0] // tasks
    for t in range(tasks):
        rows = slice(t * local, (t + 1) * local)
        both = 0.0
        for i, unit in enumerate(units):
            cols, at = block(unit, size), slice(i * size, (i + 1) * size)
            right = jnp.concatenate([w_ref[t, cols, :], mean[at, :]], axis=1)
            both = both + mat(x_ref[rows, cols], right)
        yield rows, both[:, :lanes], both[:, lanes : 2 * lanes] + both[:, 2 * lanes :]


def prepare_kernel(tasks, x_ref, *refs):
    *pieces, part_ref, w_ref, mean, sem = refs
    own, line, pairs = pieces[0], pieces[1:SIDE], pieces[SIDE:]
    blocks = [(own, 0, 0)] + [(piece, 0, k + 1) for k, piece in enumerate(line)]
    for i, pair in enumerate(pairs):
        blocks += [(pair.at[k], (1, 3)[i // 2], i % 2 * 2 + k) for k in range(2)]
    fill(w_ref, blocks, sem)
    lanes = w_ref.shape[2]
    for rows, outputs, shift in products(tasks, x_ref, w_ref, mean, units(False)):
        part_ref[rows, :lanes] = outputs
        part_ref[rows, lanes:] = shift


def first_kernel(
    scale, tasks, x_ref, squares_ref, part_ref, w_in, near_ref, wide_ref, out_ref, w_ref, mean, z, sem
):
    del w_in
    blocks = [(piece.at[k], 2, i * 2 + k) for i, piece in enumerate((near_ref, wide_ref)) for k in range(2)]
    fill(w_ref, blocks, sem)
    lanes = out_ref.shape[2]
    for rows, outputs, shift in products(tasks, x_ref, w_ref, mean, units(True)):
        outputs = outputs + part_ref[rows, :lanes]
        shift = shift + part_ref[rows, lanes:]
        high, low = split(outputs.astype(BF16).astype(F32) - shift)
        z[rows, :lanes] = high
        z[rows, lanes:] = low
    token_sums(scale, x_ref, z, out_ref)
    out_ref[:, x_ref.shape[1] // out_ref.shape[0] :] = squares_ref[...].astype(BF16)


def apply_kernel(scale, x_ref, v_ref, out_ref, u_ref, z):
    for i in range(0, x_ref.shape[0], CHUNK):
        rows = slice(i, i + CHUNK)
        u = mat(x_ref[rows, :], v_ref[...])
        u_ref[rows, :] = u
        z[:, rows] = u.T.astype(BF16)
    rows_own = x_ref.shape[1] // out_ref.shape[0]
    for j in range(0, out_ref.shape[0], 2):
        both = mat(z[...], x_ref[:, j * rows_own : (j + 2) * rows_own])
        both = (both * scale).T.astype(BF16)
        out_ref[j] = both[:rows_own]
        out_ref[j + 1] = both[rows_own:]


def sum_parts(parts_ref):
    total = parts_ref[0].astype(F32)
    for j in range(1, parts_ref.shape[0]):
        total = total + parts_ref[j].astype(F32)
    return total


def residual_kernel(total, parts_ref, w_ref, residual_ref, diag_ref, start_ref, out_ref):
    tasks, rows_own, lanes = w_ref.shape
    summed = sum_parts(parts_ref)
    columns = (summed[rows_own:] / total).T
    mean = w_ref[0].astype(F32)
    for t in range(1, tasks):
        mean = mean + w_ref[t].astype(F32)
    mean = mean / tasks
    for k, at in enumerate(range(0, rows_own, lanes)):
        rows = slice(at, min(at + lanes, rows_own))
        size = rows.stop - rows.start
        diag = jnp.zeros((size, lanes), F32)
        own = jnp.zeros((size, lanes), F32)
        for t in range(tasks):
            column = columns[:size, k * tasks + t : k * tasks + t + 1]
            diag = diag + jnp.broadcast_to(column, diag.shape)
            own = own + column * (w_ref[t, rows].astype(F32) - mean[rows])
        residual = summed[rows] + (1.0 - ALPHA) * own
        residual_ref[rows] = residual
        diag_ref[rows] = diag
        for j in range(out_ref.shape[0]):
            out_ref[j, rows] = residual.astype(BF16)
    start_ref[...] = mean


def image_kernel(parts_ref, residual_ref, diag_ref, image_ref, out_ref):
    residual = residual_ref[...]
    lost = residual - residual.astype(BF16).astype(F32)
    image = sum_parts(parts_ref) + diag_ref[...] * ((1.0 - ALPHA) * residual + ALPHA * lost)
    image_ref[...] = image
    for j in range(out_ref.shape[0]):
        out_ref[j] = image.astype(BF16)


def last_kernel(
    scale, x_ref, u_ref, r_ref, q_ref, residual_ref, image_ref, diag_ref, direction_ref, scal_ref, out_ref, v
):
    for i in range(0, x_ref.shape[0], CHUNK):
        v[i : i + CHUNK, :] = mat(x_ref[i : i + CHUNK, :], q_ref[...])
    r = r_ref[...].astype(F32)
    q = q_ref[...].astype(F32)
    norm = jnp.sum(r * r, axis=0, keepdims=True)
    alpha = norm / jnp.sum(r * q, axis=0, keepdims=True)
    r = r_ref[...].astype(F32) - alpha * q_ref[...].astype(F32)
    norm_next = jnp.sum(r * r, axis=0, keepdims=True)
    beta = norm_next / norm
    residual = residual_ref[...]
    direction = residual - alpha * image_ref[...] + beta * residual
    direction_ref[...] = direction
    scal_ref[...] = jnp.zeros_like(scal_ref)
    scal_ref[0:1, :] = alpha
    scal_ref[1:2, :] = norm_next
    shape = scal_ref.shape
    along = (1.0 + beta) * u_ref[...] - alpha * v[...]
    own = jnp.sum((diag_ref[...] * direction * direction).reshape(-1, *shape), axis=0)
    curve = scale * jnp.sum((along * along).reshape(-1, *shape), axis=0) + (1.0 - ALPHA) * own
    for j in range(out_ref.shape[0]):
        out_ref[j] = curve


def merge_kernel(parts_ref, scal_ref, start_ref, residual_ref, direction_ref, out_ref):
    curve = jnp.sum(sum_parts(parts_ref), axis=0, keepdims=True)
    out_ref[...] = (
        start_ref[...]
        + scal_ref[0:1, :] * residual_ref[...]
        + scal_ref[1:2, :] / curve * direction_ref[...]
    )


def call(kernel, name, scratch, out_shape, *args, place=pltpu.VMEM, n_vmem=1, aliases=None):
    vmem = pl.BlockSpec(memory_space=pltpu.VMEM)
    return pl.pallas_call(
        kernel,
        name=name,
        in_specs=[vmem] * n_vmem + [pl.BlockSpec(memory_space=place)] * (len(args) - n_vmem),
        out_specs=jax.tree.map(lambda _: vmem, out_shape),
        out_shape=out_shape,
        scratch_shapes=scratch,
        input_output_aliases=aliases or {},
        compiler_params=pltpu.CompilerParams(vmem_limit_bytes=10 << 20),
    )(*args)


def place():
    dp, odd = lax.axis_index("dp"), lax.axis_index("mp") % 2
    y, z = dp // SIDE, dp % SIDE
    return odd, jnp.where(odd == 0, y, z), jnp.where(odd == 0, z, y)


def owner(across, along):
    odd, at_across, at_along = place()
    a = (at_across - across + SIDE) % SIDE
    b = (at_along - along + SIDE) % SIDE
    return jnp.where(odd == 0, a * SIDE + b, b * SIDE + a)


def units(late):
    odd, across, _ = place()
    far = (across + 2) % SIDE
    even_units = []
    for base in (across, far) if late else ((across + 1) % SIDE, (across + 3) % SIDE):
        even_units += [2 * base, 2 * base + 1]
    pair = far // 2 if late else 1 - far // 2
    return [jnp.where(odd == 0, even_units[i], 2 * i + pair) for i in range(SIDE)]


def send(value, n_cols, across, along):
    pairs = []
    for dp in range(SIDE * SIDE):
        for mp in range(n_cols):
            step_y, step_z = (across, along) if mp % 2 == 0 else (along, across)
            y, z = (dp // SIDE + step_y) % SIDE, (dp % SIDE + step_z) % SIDE
            pairs.append((dp * n_cols + mp, (y * SIDE + z) * n_cols + mp))
    return lax.ppermute(value, ALL, pairs)


def shards(activations, task_weights):
    tasks, local, width = activations.shape
    lanes = task_weights.shape[2]
    n_rows, n_cols = lax.axis_size("dp"), lax.axis_size("mp")
    rows_own = width // n_rows
    tokens = tasks * local
    total = tokens * n_rows

    def exchange(value):
        return lax.all_to_all(value, "dp", 0, 0, tiled=False)

    scale = ALPHA / total
    unit = pltpu.VMEM((width // 2, 2 * lanes), BF16)
    halves = pltpu.VMEM((tokens, 2 * lanes), BF16)
    rows = jax.ShapeDtypeStruct((rows_own, lanes), F32)
    copies = jax.ShapeDtypeStruct((n_rows, rows_own, lanes), BF16)
    small = jax.ShapeDtypeStruct((8, lanes), F32)
    extra = 2 * 8
    line = [send(task_weights, n_cols, 0, k) for k in range(1, SIDE)]
    vmem = pl.BlockSpec(memory_space=pltpu.VMEM)
    x, squares = pl.pallas_call(
        load_kernel,
        name="load",
        in_specs=[pl.BlockSpec(memory_space=pltpu.HBM)],
        out_specs=(vmem, vmem),
        out_shape=(
            pltpu.VMEM((tokens, width), BF16),
            jax.ShapeDtypeStruct((n_rows, extra, lanes), F32),
        ),
        scratch_shapes=[pltpu.VMEM((tasks, width), F32), pltpu.SemaphoreType.DMA((tasks,))],
        compiler_params=pltpu.CompilerParams(vmem_limit_bytes=4 << 20),
    )(pltpu.with_memory_space_constraint(activations, pltpu.HBM))
    *line, squares = lax.optimization_barrier((*line, squares))
    near, wide = jnp.stack([task_weights, line[0]]), jnp.stack(line[1:])
    left_near = send(near, n_cols, 1, 0)
    right_wide = send(wide, n_cols, 3, 0)
    left_wide = send(wide, n_cols, 1, 0)
    right_near = send(near, n_cols, 3, 0)
    far_near = send(left_near, n_cols, 1, 0)
    far_wide = send(right_wide, n_cols, 3, 0)
    part, w = call(
        functools.partial(prepare_kernel, tasks),
        "prepare",
        [unit, pltpu.SemaphoreType.DMA((n_rows - SIDE,))],
        (
            jax.ShapeDtypeStruct((tokens, 2 * lanes), F32),
            jax.ShapeDtypeStruct((tasks, width, lanes), BF16),
        ),
        x,
        task_weights,
        *line,
        left_near,
        left_wide,
        right_near,
        right_wide,
        place=pl.ANY,
    )
    part, _ = call(
        functools.partial(first_kernel, scale, tasks),
        "first",
        [unit, halves, pltpu.SemaphoreType.DMA((SIDE,))],
        (
            jax.ShapeDtypeStruct((n_rows, rows_own + extra, lanes), BF16),
            jax.ShapeDtypeStruct((tasks, width, lanes), BF16),
        ),
        x,
        squares,
        part,
        w,
        far_near,
        far_wide,
        place=pl.ANY,
        n_vmem=4,
        aliases={3: 1},
    )
    residual, diag, start, sent = call(
        functools.partial(residual_kernel, total),
        "residual",
        [],
        (rows, rows, rows, copies),
        exchange(part),
        task_weights,
    )
    r_full = exchange(sent).reshape(width, lanes)
    part, u = call(
        functools.partial(apply_kernel, scale),
        "apply",
        [pltpu.VMEM((lanes, tokens), BF16)],
        (copies, jax.ShapeDtypeStruct((tokens, lanes), F32)),
        x,
        r_full,
    )
    image, sent = call(image_kernel, "image", [], (rows, copies), exchange(part), residual, diag)
    q_full = exchange(sent).reshape(width, lanes)
    direction, scal, curve = call(
        functools.partial(last_kernel, scale),
        "last",
        [pltpu.VMEM((tokens, lanes), F32)],
        (rows, small, jax.ShapeDtypeStruct((n_rows, 8, lanes), F32)),
        x,
        u,
        r_full,
        q_full,
        residual,
        image,
        diag,
    )
    return call(
        merge_kernel, "merge", [], rows, exchange(curve), scal, start, residual, direction
    )


def solution(mesh):
    return jax.shard_map(
        shards,
        mesh=mesh,
        in_specs=(P(None, "dp", None), P(None, "dp", "mp")),
        out_specs=P("dp", "mp"),
        check_vma=False,
    )
```
